512 devices in a mesh: dir: 8 (over x, core), texel: 64 (over z, y).
Axes of the slice: x: 4, y: 4, z: 16, core: 2. Of those that a mesh axis runs over, the one named last changes fastest.
Arguments:
- texels: bfloat16 [4096, 50176], P('texel', 'dir'), may hold values from -6 to 6
- labels: int32 [4096, 1], P('texel'), may hold values from 0 to 127; in each aligned block of 64 rows (0 to 63, 64 to 127, ...) at most 2 rows name the same one
- start_basis: bfloat16 [64, 50176], P(None, 'dir'), may hold values from -0.02734375 to 0.02734375
Outputs:
- coefficients: float32 [4096, 64], P('texel')
- bases: bfloat16 [128, 64, 50176], P('texel', None, 'dir')
The draws below stay inside these ranges and needn't reach their ends.
Inputs may be any that keep to these rules, and one draw needn't show every extreme that they name: `labels`: among the rows of one index of texel (an aligned block of 64 rows) no cluster is named by more than 2 rows, a bound that some block reaches in every draw.
All inputs are finite; a program needn't handle non-finite values.
Results may differ from the reference program's by a relative error of at most 0.012.
Values may be sent and summed in bfloat16 or wider, within the bound.
A program may use at most 64 MiB of HBM per device.

```python
import math
import jax
import jax.numpy as jnp
import numpy as np
from jax import lax

COLS = 50176
K = 64
ROWS_DEV = 64
CAP = 2
ITERS = 2
CLUSTERS = 128
TEXELS = 4096
N_TEXEL = 64


def block_levels(own_key, extent, shards, low, largest):
    factor_of = 1.0
    for dim, parts in shards:
        heights = jax.random.uniform(jax.random.fold_in(jax.random.fold_in(own_key, 6), dim), (parts,), jnp.float32, low / len(shards), largest / len(shards))
        factor_of = factor_of * jnp.repeat(jnp.exp(heights), extent[dim] // parts).reshape((-1,) + (1,) * (len(extent) - 1 - dim))
    return factor_of


def shared_out(rng, own, number, rows, count, top, most, lean):
    ranking = jax.random.permutation(rng, count)
    heavy_load, usual = load_shares(count, rows * top, most, lean, True), load_shares(count, rows * top, most, lean, False)
    places = jnp.arange(count)

    def named(sizes, offset_by):
        used = int((sizes > 0).sum())
        fixed = max(1, used // 4)
        moved = fixed + (places - fixed + offset_by * (used - fixed)) % max(1, count - fixed)
        return jnp.zeros((count,), jnp.int32).at[ranking[jnp.where(places < fixed, places, moved)]].set(jnp.asarray(sizes, jnp.int32))

    sizes = jnp.where(number % 4 == 0, named(heavy_load, number // 4), named(usual, number - number // 4 - 1))
    mixed = jax.random.permutation(jax.random.fold_in(own, 3), count)
    giver, taker = mixed[0:count // 2 * 2:2], mixed[1:count // 2 * 2:2]
    margin = jnp.minimum(sizes[giver] - 1, most - sizes[taker]) // 2
    margin = jnp.where((giver == ranking[0]) | (taker == ranking[0]) | (sizes[taker] == 0), 0, jnp.maximum(margin, 0))
    moved = jax.random.randint(jax.random.fold_in(own, 4), (count // 2,), 0, 1 << 20) % (margin + 1)
    sizes = sizes.at[giver].add(-moved).at[taker].add(moved)
    members = jnp.searchsorted(jnp.cumsum(sizes), jnp.arange(rows * top), side="right").astype(jnp.int32)
    grid = members.reshape(top, rows).T
    grid = grid[jax.random.permutation(jax.random.fold_in(own, 1), rows)]
    offset_by = jax.random.randint(jax.random.fold_in(own, 2), (rows, 1), 0, top)
    return jnp.take_along_axis(grid, (jnp.arange(top)[None, :] + offset_by) % top, axis=1)


def load_shares(amount, total, reach, lean, full):
    loads = [(1 << 20) // math.isqrt(standing ** lean) + 1 for standing in range(1, amount + 1)]
    largest = reach if full else min(reach, max(-(-total // amount), total * loads[0] // sum(loads)))
    least = 1 if total - largest >= amount - 1 else 0
    holding, surplus = [largest] + [least] * (amount - 1), total - largest - least * (amount - 1)
    while surplus > 0:
        candidates = [i for i in range(1, amount) if holding[i] < largest] or [i for i in range(1, amount) if holding[i] < reach]
        pool, left = sum([loads[i] for i in candidates]), surplus
        for i in candidates:
            addition = min(reach - holding[i], max(1, left * loads[i] // pool), surplus)
            holding[i] = holding[i] + addition
            surplus = surplus - addition
    return np.array(holding)


def gaussian(own_key, dims, width, limit, shards=(), kind=jnp.bfloat16):
    result = jax.random.normal(own_key, dims, jnp.float32) * width
    if len(shards) > 0:
        result = block_levels(own_key, dims, shards, -0.22, 0.18) * result
    return jnp.clip(result, min=-limit, max=limit).astype(kind)


def setup_inputs(seed: int = 0) -> dict:
    seeds = jax.random.split(jax.random.key(seed), 4)
    texels = gaussian(seeds[0], (TEXELS, COLS), 1.0, 6.0, ((0, 64), (1, 8)))
    labels_keys = jax.random.split(jax.random.fold_in(seeds[1], 1), TEXELS // ROWS_DEV)
    labels_turns = jax.random.permutation(jax.random.fold_in(seeds[1], 3), TEXELS // ROWS_DEV)
    labels = jax.vmap(lambda own, number: shared_out(jax.random.fold_in(seeds[1], 2), own, number, ROWS_DEV, CLUSTERS, 1, CAP, 2))(labels_keys, labels_turns).reshape((TEXELS, 1))
    start_basis = gaussian(seeds[2], (K, COLS), COLS ** -0.5, 0.02734375, ((1, 8),))
    return {"texels": texels, "labels": labels, "start_basis": start_basis}


ridge_share = 0.05

def reference(texels, labels, start_basis):
    label_col = labels[:, 0].astype(jnp.int32)
    texel_count = label_col.shape[0]
    sorted_rows = jnp.argsort(label_col, stable=True).astype(jnp.int32)
    cluster_ids = jnp.arange(CLUSTERS, dtype=jnp.int32)
    counts = jnp.sum((label_col[None, :] == cluster_ids[:, None]).astype(jnp.int32), axis=1)
    starts = (jnp.cumsum(counts) - counts).astype(jnp.int32)
    capacity = N_TEXEL * CAP
    ridge_term = jnp.float32(ridge_share * COLS)
    identity = jnp.eye(K, dtype=jnp.float32)

    def per_cluster(cluster):
        offsets = jnp.arange(capacity, dtype=jnp.int32)
        is_live = offsets < counts[cluster]
        picked = jnp.clip(starts[cluster] + offsets, 0, texel_count - 1).astype(jnp.int32)
        row_block = jnp.take(texels, sorted_rows[picked], axis=0)
        row_block = jnp.where(is_live[:, None], row_block, jnp.zeros_like(row_block))
        basis_now = start_basis
        for sweep in range(ITERS):
            projected = jnp.dot(row_block.astype(jnp.float32), basis_now.T.astype(jnp.float32), preferred_element_type=jnp.float32).astype(jnp.bfloat16)
            widened = jnp.dot(projected.T.astype(jnp.float32), row_block.astype(jnp.float32), preferred_element_type=jnp.float32) + ridge_term * basis_now.astype(jnp.float32)
            gram_mat = jnp.dot(widened.astype(jnp.float32), widened.T.astype(jnp.float32), precision=lax.Precision.HIGHEST, preferred_element_type=jnp.float32)
            lower_tri = jnp.linalg.cholesky(gram_mat)
            inverse = jax.scipy.linalg.solve_triangular(lower_tri, identity, lower=True)
            basis_now = jnp.dot(inverse.astype(jnp.float32), widened.astype(jnp.float32), precision=lax.Precision.HIGHEST, preferred_element_type=jnp.float32).astype(jnp.bfloat16)
        coef_rows = jnp.dot(row_block.astype(jnp.float32), basis_now.T.astype(jnp.float32), preferred_element_type=jnp.float32)
        return (basis_now, coef_rows)
    bases, coef_all = lax.map(per_cluster, cluster_ids)
    position = jnp.zeros((texel_count,), jnp.int32).at[sorted_rows].set(jnp.arange(texel_count, dtype=jnp.int32))
    slot_rank = (position - starts[label_col]).astype(jnp.int32)
    coefficients = coef_all[label_col, slot_rank]
    return (coefficients, bases)
```

```python
import jax
import jax.numpy as jnp
from jax import lax
from jax.experimental import pallas as pl
from jax.experimental.pallas import tpu as pltpu
from jax.sharding import PartitionSpec as P

COLS = 50176
K = 64
CL_DEV = 2
ITERS = 2
RIDGE = 0.05 * COLS
HIGHEST = lax.Precision.HIGHEST


def mm(a, b):
    return jnp.dot(a, b, precision=HIGHEST, preferred_element_type=jnp.float32)


def mm_t(a, b):
    return lax.dot_general(
        a, b, (((1,), (1,)), ((), ())), precision=HIGHEST, preferred_element_type=jnp.float32
    )


def inverse_cholesky(grams):
    rows = lax.broadcasted_iota(jnp.int32, (K, 2 * K), 0)
    lanes = lax.broadcasted_iota(jnp.int32, (K, 2 * K), 1)
    eye = (lax.broadcasted_iota(jnp.int32, (K, K), 0) == lax.broadcasted_iota(jnp.int32, (K, K), 1)).astype(jnp.float32)
    work = [jnp.concatenate([g, eye], axis=1) for g in grams]
    for j in range(K - 1):
        for c in range(len(work)):
            a = work[c]
            row = a[j : j + 1, :]
            scaled = row * (1.0 / a[j : j + 1, j : j + 1])
            col = jnp.where(rows > j, jnp.broadcast_to(a[:, j : j + 1], (K, 2 * K)), 0.0)
            work[c] = a - col * scaled
    out = []
    for a in work:
        pivots = jnp.sum(jnp.where(rows == lanes, a, 0.0), axis=1, keepdims=True)
        out.append(a[:, K:] * (1.0 / jnp.sqrt(pivots)))
    return out


def update_kernel(gram_ref, rows_ref, start_ref, basis_ref, coef_ref):
    cl = range(CL_DEV)
    n = rows_ref.shape[1]
    base = CL_DEV * n
    g = [gram_ref[c * n : (c + 1) * n, :] for c in cl]
    pt = [gram_ref[base + c * K : base + (c + 1) * K, :] for c in cl]
    p = [jnp.transpose(pt[c]) for c in cl]
    s = gram_ref[base + CL_DEV * K :, :K]
    ridge = jnp.float32(RIDGE)
    gram1 = [
        mm_t(mm(pt[c], g[c]), pt[c]) + (2.0 * ridge) * mm_t(pt[c], pt[c]) + (ridge * ridge) * s
        for c in cl
    ]
    inv1 = inverse_cholesky(gram1)
    a1 = [mm(inv1[c], pt[c]) for c in cl]
    b1 = [ridge * inv1[c] for c in cl]
    p2t = [mm(a1[c], g[c]) + mm(b1[c], pt[c]) for c in cl]
    wa = [p2t[c] + ridge * a1[c] for c in cl]
    wb = [ridge * b1[c] for c in cl]
    yr = [mm(wa[c], g[c]) + mm(wb[c], pt[c]) for c in cl]
    ys = [mm(wa[c], p[c]) + mm(wb[c], s) for c in cl]
    gram2 = [mm_t(yr[c], wa[c]) + mm_t(ys[c], wb[c]) for c in cl]
    inv2 = inverse_cholesky(gram2)
    for c in cl:
        a2 = mm(inv2[c], wa[c])
        b2 = mm(inv2[c], wb[c])
        coef_ref[c] = jnp.transpose(mm(a2, g[c]) + mm(b2, pt[c])).astype(coef_ref.dtype)
        a_hi = a2.astype(jnp.bfloat16)
        a_lo = (a2 - a_hi.astype(jnp.float32)).astype(jnp.bfloat16)
        b_hi = b2.astype(jnp.bfloat16)
        b_lo = (b2 - b_hi.astype(jnp.float32)).astype(jnp.bfloat16)
        width = basis_ref.shape[2] // 7
        for w in range(7):
            cols = slice(w * width, (w + 1) * width)
            r = rows_ref[c, :, cols]
            b = start_ref[:, cols]
            f32 = jnp.float32
            acc = jnp.dot(a_hi, r, preferred_element_type=f32) + jnp.dot(a_lo, r, preferred_element_type=f32)
            acc += jnp.dot(b_hi, b, preferred_element_type=f32) + jnp.dot(b_lo, b, preferred_element_type=f32)
            basis_ref[c, :, cols] = acc.astype(basis_ref.dtype)


def update(gram, rows, start):
    c, r, w = rows.shape
    vmem = pl.BlockSpec(memory_space=pltpu.VMEM)
    return pl.pallas_call(
        update_kernel,
        name="update",
        out_shape=(
            jax.ShapeDtypeStruct((c, K, w), jnp.bfloat16),
            jax.ShapeDtypeStruct((c, r, K), jnp.bfloat16),
        ),
        in_specs=[vmem] * 3,
        out_specs=(vmem, vmem),
        compiler_params=pltpu.CompilerParams(vmem_limit_bytes=48 * 1024 * 1024),
    )(gram, rows, start)


def per_device(texels, labels, start_basis):
    row_count = texels.shape[0]
    col_width = texels.shape[1]
    groups = lax.axis_size("texel")
    slot_cap = max(2, 2 * row_count // (CL_DEV * groups))
    label_col = labels[:, 0]
    owners = label_col // CL_DEV
    local_idx = label_col % CL_DEV
    row_ids = jnp.arange(row_count, dtype=jnp.int32)
    matches = (label_col[None, :] == label_col[:, None]) & (row_ids[None, :] < row_ids[:, None])
    slot_rank = jnp.sum(matches.astype(jnp.int32), axis=1)
    slot_of_row = local_idx * (groups * slot_cap) + owners * slot_cap + slot_rank
    total_slots = CL_DEV * groups * slot_cap
    slot_ids = jnp.arange(total_slots, dtype=jnp.int32)
    slot_hit = slot_of_row[None, :] == slot_ids[:, None]
    pick = slot_hit.astype(jnp.bfloat16)
    outgoing = jnp.dot(pick, texels, preferred_element_type=jnp.float32).astype(jnp.bfloat16)
    outgoing = outgoing.reshape(CL_DEV, groups * slot_cap, col_width)
    received = lax.all_to_all(outgoing, "texel", split_axis=1, concat_axis=1, tiled=True)
    f32 = jnp.float32
    grr = jnp.einsum("crw,csw->crs", received, received, preferred_element_type=f32)
    gsr = jnp.einsum("kw,crw->ckr", start_basis, received, preferred_element_type=f32)
    gss = jnp.einsum("jw,kw->jk", start_basis, start_basis, preferred_element_type=f32)
    n = received.shape[1]
    parts = (grr.reshape(CL_DEV * n, n), gsr.reshape(CL_DEV * K, n), jnp.pad(gss, ((0, 0), (0, n - K))))
    gram = lax.psum(jnp.concatenate(parts, axis=0), "dir")
    basis, summed = update(gram, received, start_basis)
    returned = lax.all_to_all(summed, "texel", split_axis=1, concat_axis=1, tiled=True)
    returned = returned.reshape(total_slots, K)
    coefficients = jnp.dot(pick.T, returned, preferred_element_type=f32)
    return (coefficients, basis)


def solution(mesh):
    in_specs = (P("texel", "dir"), P("texel", None), P(None, "dir"))
    out_specs = (P("texel", None), P("texel", None, "dir"))
    return jax.shard_map(
        per_device, mesh=mesh, in_specs=in_specs, out_specs=out_specs, check_vma=False
    )
```
